128 devices in a mesh: cfg: 2 (over x_lo), seq: 32 (over y, z, core), req: 2 (over x_hi).
Axes of the slice: x: 4 (x_hi: 2, x_lo: 2; x = x_hi * 2 + x_lo), y: 4, z: 4, core: 2. Of those that a mesh axis runs over, the one named last changes fastest.
Arguments:
- latents: float32 [4096, 8, 64], P('seq', 'req', 'cfg'), may hold values from -6 to 6
- hidden_img: bfloat16 [2, 4096, 8, 3072], P('cfg', 'seq', 'req'), may hold values from -3 to 3
- query_img: bfloat16 [2, 4096, 8, 2048], P('cfg', 'seq', 'req'), may hold values from -12 to 12
- key_img: bfloat16 [2, 4096, 8, 2048], P('cfg', 'seq', 'req'), may hold values from -12 to 12
- value_img: bfloat16 [2, 4096, 8, 2048], P('cfg', 'seq', 'req'), may hold values from -6 to 6
- key_txt: bfloat16 [2, 512, 8, 2048], P('cfg', 'seq', 'req'), may hold values from -12 to 12
- value_txt: bfloat16 [2, 512, 8, 2048], P('cfg', 'seq', 'req'), may hold values from -6 to 6
- text_len: int32 [2, 8], P('cfg', 'req'), may hold values from 1 to 512, 2048 in all within a row
- img_ids: int32 [3, 4096], P(None, 'seq'), may hold values from 0 to 63
- t_index: int32 [8], P('req'), may hold values from 1 to 28
- g_index: int32 [8], P('req'), may hold values from 0 to 8
- proj_weight: bfloat16 [2048, 3072], P(('cfg', 'seq')), may hold values from -0.125 to 0.125
- attn_gate: float32 [2, 8, 3072], P('cfg', 'req'), may hold values from -4 to 4
- final_shift: float32 [2, 8, 3072], P('cfg', 'req'), may hold values from -3 to 3
- final_scale: float32 [2, 8, 3072], P('cfg', 'req'), may hold values from -2 to 2
- out_weight: bfloat16 [3072, 64], replicated, may hold values from -0.109375 to 0.109375
- out_bias: float32 [64], replicated, may hold values from -3 to 3
Outputs:
- next_latents: float32 [4096, 8, 64], P('seq', 'req', 'cfg')
- denoised: float32 [4096, 8, 64], P('seq', 'req', 'cfg')
The draws below stay inside these ranges and needn't reach their ends.
Inputs may be any that keep to these rules, and one draw needn't show every extreme that they name: `text_len`: in each half the lengths of all 8 prompts sum to 2048 and the largest is 512.
All inputs are finite; a program needn't handle non-finite values. No bound on the sum of `text_len` on one device may be relied on, other than what follows from the above.
Results may differ from the reference program's by a relative error of at most 0.0066.
Values may be sent and summed in bfloat16 or wider, within the bound.
A program may use at most 128 MiB of HBM per device.

```python
import math
import jax
import jax.numpy as jnp
import numpy as np
from jax import lax

D = 3072
HEADS = 16
HSIZE = 128
CH = 64
STEPS = 28
PROMPTS = 8
IMG = 4096
TXT = 512
HD = 2048


def still_entries():
    rate_list = []
    for extent in (HSIZE // 8, 7 * HSIZE // 16, 7 * HSIZE // 16):
        for pair_index in range(extent // 2):
            rate_list.append(10000.0 ** (-2.0 * pair_index / extent))
    still_pairs = np.array([63.0 * rate_value <= 0.05 for rate_value in rate_list])
    return np.concatenate([still_pairs, still_pairs])


def drawn_plan(key):
    plan_key = jax.random.fold_in(key, 7001)
    sign_key, place_key, level_key = jax.random.split(plan_key, 3)
    signs = (2 * jax.random.randint(sign_key, (2, PROMPTS, HEADS, HSIZE), 0, 2) - 1).astype(jnp.float32)
    places = jax.random.randint(place_key, (2, PROMPTS, HEADS), 0, IMG // 2)
    offsets = jax.random.randint(level_key, (2, PROMPTS, 1), 0, 4)
    level_index = (jnp.arange(HEADS, dtype=jnp.int32)[None, None, :] + offsets) % 4
    level_table = jnp.array([7.0, 9.0, 10.5, 12.0], jnp.float32)
    levels = jnp.take(level_table, level_index)
    return (signs, places, levels)


def draw_query_img(key, part):
    field_key = jax.random.fold_in(key, 7002)
    shape = (2, IMG, PROMPTS, HEADS, HSIZE)
    base = jnp.clip(2.0 * jax.random.normal(field_key, shape, jnp.float32), -12.0, 12.0)
    signs, places, levels = drawn_plan(key)
    still = jnp.asarray(still_entries())
    tokens = jnp.arange(IMG, dtype=jnp.int32)[None, :, None, None]
    chosen = (tokens == places[:, None, :, :])[..., None]
    pattern = jnp.where(still, levels[..., None] * signs, 0.0)
    result = jnp.where(chosen, pattern[:, None], base)
    return result.reshape(2, IMG, PROMPTS, HD).astype(jnp.bfloat16)


def draw_key_img(key, part):
    field_key = jax.random.fold_in(key, 7003)
    shape = (2, IMG, PROMPTS, HEADS, HSIZE)
    base = jnp.clip(2.0 * jax.random.normal(field_key, shape, jnp.float32), -12.0, 12.0)
    signs, places, levels = drawn_plan(key)
    still_table = still_entries()
    still = jnp.asarray(still_table)
    first_still = int(np.argmax(still_table))
    tokens = jnp.arange(IMG, dtype=jnp.int32)[None, :, None, None]
    own_rows = (tokens == places[:, None, :, :])[..., None]
    far_rows = (tokens == places[:, None, :, :] + IMG // 2)[..., None]
    pattern = levels[..., None] * signs
    lowered_step = 2.0 * math.sqrt(HSIZE) / levels
    entry_mark = (jnp.arange(HSIZE, dtype=jnp.int32) == first_still).astype(jnp.float32)
    lowered = pattern - lowered_step[..., None] * entry_mark * signs
    with_own = jnp.where(own_rows & still, pattern[:, None], base)
    result = jnp.where(far_rows & still, lowered[:, None], with_own)
    return result.reshape(2, IMG, PROMPTS, HD).astype(jnp.bfloat16)


def touch_ends(values, own_key, least, largest):
    dims = values.shape
    spot = [jax.random.randint(jax.random.fold_in(own_key, axis), (), 0, dims[axis]) for axis in range(len(dims))]
    values = values.at[tuple(spot)].set(least)
    longest = dims.index(max(dims))
    spot[longest] = (spot[longest] + 1) % dims[longest]
    return values.at[tuple(spot)].set(largest)


def block_scale(own_key, dims, cuts, smallest, top_value):
    def one(axis_at, parts):
        steps = jax.random.uniform(jax.random.fold_in(jax.random.fold_in(own_key, 6), axis_at), (parts,), jnp.float32, smallest / len(cuts), top_value / len(cuts))
        return jnp.repeat(jnp.exp(steps), dims[axis_at] // parts).reshape((-1,) + (1,) * (len(dims) - axis_at - 1))

    level = one(*cuts[0])
    for cut in cuts[1:]:
        level = level * one(*cut)
    return level


def length_profile(number_of, total, most, slope):
    weights = [(1 << 20) // math.isqrt(grade ** slope) + 1 for grade in range(2, number_of + 1)]
    spare, holding = total - most - (number_of - 1), [1] * (number_of - 1)
    while spare > 0:
        movable = [i for i in range(number_of - 1) if holding[i] < most]
        mass, left = sum([weights[i] for i in movable]), spare
        for i in movable:
            addition = min(most - holding[i], max(1, left * weights[i] // mass), spare)
            holding[i] = holding[i] + addition
            spare = spare - addition
    return np.array([most] + holding)


def uneven(key, number_of, total, bound, skew):
    if number_of == 2:
        one = jax.random.randint(key, (), max(1, total - bound), min(bound, total - 1) + 1)
        return jnp.stack([one, total - one])
    lengths = jnp.asarray(length_profile(number_of, total, bound, skew), jnp.int32)
    pairs = (number_of - 1) // 2
    giver, receiver = lengths[1:1 + 2 * pairs:2], lengths[2:2 + 2 * pairs:2]
    slack = jnp.minimum(giver - 1, bound - receiver)
    passed = jax.random.randint(jax.random.fold_in(key, 1), (pairs,), 0, 1 << 20) % (slack + 1)
    lengths = lengths.at[1:1 + 2 * pairs:2].set(giver - passed).at[2:2 + 2 * pairs:2].set(receiver + passed)
    return lengths[jax.random.permutation(jax.random.fold_in(key, 2), number_of)]


def normal_values(rng, shape, deviation, limit, cuts=(), kind=jnp.bfloat16):
    factor_of = block_scale(rng, shape, cuts, -0.22, 0.18) if cuts else 1.0
    entries = jax.random.normal(rng, shape, jnp.float32) * deviation * factor_of
    return jnp.minimum(jnp.maximum(entries, -limit), limit).astype(kind)


def setup_inputs(seed: int = 0) -> dict:
    splits = jax.random.split(jax.random.key(seed), 18)
    latents = normal_values(splits[0], (IMG, PROMPTS, CH), 1.0, 6.0, ((0, 32), (1, 2), (2, 2)), jnp.float32)
    hidden_img = normal_values(splits[1], (2, IMG, PROMPTS, D), 0.5, 3.0, ((0, 2), (1, 32), (2, 2)))
    query_img = draw_query_img(jax.random.fold_in(splits[17], 71), 0)
    key_img = draw_key_img(jax.random.fold_in(splits[17], 71), 0)
    value_img = normal_values(splits[4], (2, IMG, PROMPTS, HD), 1.0, 6.0, ((0, 2), (1, 32), (2, 2)))
    key_txt = normal_values(splits[5], (2, TXT, PROMPTS, HD), 2.0, 12.0, ((0, 2), (1, 32), (2, 2)))
    value_txt = normal_values(splits[6], (2, TXT, PROMPTS, HD), 1.0, 6.0, ((0, 2), (1, 32), (2, 2)))
    text_len = jax.vmap(lambda own: uneven(own, PROMPTS, TXT * PROMPTS // 2, TXT, 1))(jax.random.split(splits[7], 2)).reshape((2, PROMPTS)).astype(jnp.int32)
    img_ids = touch_ends(jax.random.randint(splits[8], (3, IMG), 0, 64), jax.random.fold_in(splits[8], 1), 0, 63).astype(jnp.int32)
    t_index = touch_ends(jax.random.randint(splits[9], (PROMPTS,), 1, STEPS + 1), jax.random.fold_in(splits[9], 1), 1, STEPS).astype(jnp.int32)
    g_index = touch_ends(jax.random.randint(splits[10], (PROMPTS,), 0, 9), jax.random.fold_in(splits[10], 1), 0, 8).astype(jnp.int32)
    proj_weight = normal_values(splits[11], (HD, D), HD ** -0.5, 0.125, ((0, 64),))
    attn_gate = normal_values(splits[12], (2, PROMPTS, D), 1.0, 4.0, ((0, 2), (1, 2)), jnp.float32)
    final_shift = normal_values(splits[13], (2, PROMPTS, D), 0.5, 3.0, ((0, 2), (1, 2)), jnp.float32)
    final_scale = normal_values(splits[14], (2, PROMPTS, D), 0.3, 2.0, ((0, 2), (1, 2)), jnp.float32)
    out_weight = normal_values(splits[15], (D, CH), D ** -0.5, 0.109375)
    out_bias = normal_values(splits[16], (CH,), 0.5, 3.0, (), jnp.float32)
    return {"latents": latents, "hidden_img": hidden_img, "query_img": query_img, "key_img": key_img, "value_img": value_img, "key_txt": key_txt, "value_txt": value_txt, "text_len": text_len, "img_ids": img_ids, "t_index": t_index, "g_index": g_index, "proj_weight": proj_weight, "attn_gate": attn_gate, "final_shift": final_shift, "final_scale": final_scale, "out_weight": out_weight, "out_bias": out_bias}


def rope_angles(position_ids):
    pieces = []
    for axis_number, extent in enumerate((HSIZE // 8, 7 * HSIZE // 16, 7 * HSIZE // 16)):
        freq = jnp.power(jnp.float32(10000.0), -2.0 * jnp.arange(extent // 2, dtype=jnp.float32) / extent)
        pieces.append(position_ids[axis_number].astype(jnp.float32)[:, None] * freq[None, :])
    return jnp.concatenate(pieces, axis=1)

def rotate(values, angle):
    half_width = values.shape[-1] // 2
    first = values[..., :half_width]
    second = values[..., half_width:]
    cosine = jnp.cos(angle)
    sine = jnp.sin(angle)
    return jnp.concatenate([first * cosine - second * sine, first * sine + second * cosine], axis=-1)

def attend(queries, keys_img, values_img, keys_txt, values_txt, length):
    factor = HSIZE ** (-0.5)
    score_img = jnp.dot(queries, keys_img.T, preferred_element_type=jnp.float32) * factor
    score_txt = jnp.dot(queries, keys_txt.T, preferred_element_type=jnp.float32) * factor
    live = jnp.arange(keys_txt.shape[0], dtype=jnp.int32) < length
    score_txt = jnp.where(live[None, :], score_txt, jnp.float32(-1e+30))
    top = jnp.maximum(lax.optimization_barrier(jnp.max(score_img, axis=1)), lax.optimization_barrier(jnp.max(score_txt, axis=1)))
    exp_img = jnp.exp(score_img - top[:, None])
    exp_txt = jnp.where(live[None, :], jnp.exp(score_txt - top[:, None]), jnp.float32(0.0))
    total = lax.optimization_barrier(jnp.sum(exp_img, axis=1)) + lax.optimization_barrier(jnp.sum(exp_txt, axis=1))
    summed = jnp.dot(exp_img.astype(jnp.bfloat16), values_img, preferred_element_type=jnp.float32)
    summed = summed + jnp.dot(exp_txt.astype(jnp.bfloat16), values_txt, preferred_element_type=jnp.float32)
    return (summed / total[:, None]).astype(jnp.bfloat16)

def roster(fraction):
    return 3.0 * fraction / (1.0 + 2.0 * fraction)

def final_layer(residual, shift, scale, out_weight, out_bias):
    mean_value = lax.optimization_barrier(jnp.mean(residual, axis=-1, keepdims=True))
    centred = residual - mean_value
    spread = lax.optimization_barrier(jnp.mean(centred * centred, axis=-1, keepdims=True))
    normed = centred * lax.rsqrt(spread + 1e-06)
    modulated = (normed * (1.0 + scale) + shift).astype(jnp.bfloat16)
    rows = modulated.reshape(-1, modulated.shape[-1])
    velocity = jnp.dot(rows, out_weight, preferred_element_type=jnp.float32) + out_bias[None, :]
    return velocity

def reference(latents, hidden_img, query_img, key_img, value_img, key_txt, value_txt, text_len, img_ids, t_index, g_index, proj_weight, attn_gate, final_shift, final_scale, out_weight, out_bias):
    angle = rope_angles(img_ids)[:, None, :]
    members = PROMPTS * HEADS
    velocities = []
    for half in range(2):
        rot_query = rotate(query_img[half].reshape(IMG, members, HSIZE).astype(jnp.float32), angle).astype(jnp.bfloat16)
        rot_key = rotate(key_img[half].reshape(IMG, members, HSIZE).astype(jnp.float32), angle).astype(jnp.bfloat16)
        vals = value_img[half].reshape(IMG, members, HSIZE)
        text_keys = key_txt[half].reshape(TXT, members, HSIZE)
        text_vals = value_txt[half].reshape(TXT, members, HSIZE)
        member_len = jnp.repeat(text_len[half], HEADS)

        def one_member(packed):
            return attend(packed[0], packed[1], packed[2], packed[3], packed[4], packed[5])
        attended = lax.map(one_member, (jnp.moveaxis(rot_query, 1, 0), jnp.moveaxis(rot_key, 1, 0), jnp.moveaxis(vals, 1, 0), jnp.moveaxis(text_keys, 1, 0), jnp.moveaxis(text_vals, 1, 0), member_len))
        attended = jnp.moveaxis(attended, 0, 1).reshape(IMG * PROMPTS, HD)
        projected = jnp.dot(attended, proj_weight, preferred_element_type=jnp.float32).reshape(IMG, PROMPTS, D)
        residual = hidden_img[half].astype(jnp.float32) + attn_gate[half][None] * projected
        velocity = final_layer(residual, final_shift[half][None], final_scale[half][None], out_weight, out_bias)
        velocities.append(velocity.reshape(IMG, PROMPTS, CH))
    strength = (1.0 + 0.5 * g_index.astype(jnp.float32))[None, :, None]
    guided = velocities[1] + strength * (velocities[0] - velocities[1])
    moment = t_index.astype(jnp.float32)
    sigma_now = roster(moment / STEPS)[None, :, None]
    sigma_next = roster((moment - 1.0) / STEPS)[None, :, None]
    next_latents = latents + (sigma_next - sigma_now) * guided
    denoised = latents - sigma_now * guided
    return (next_latents, denoised)
```

```python
import functools
import math

import jax
import jax.numpy as jnp
from jax import lax
from jax.experimental import pallas as pl
from jax.experimental.pallas import tpu as pltpu
from jax.sharding import PartitionSpec as P

HSIZE = 128
STEPS = 28
QBLOCK = 512
KBLOCK = 512


def partner_2(value, axis, distance):
    mask = 2**distance
    pairs = [(source, source ^ mask) for source in range(lax.axis_size(axis))]
    return lax.ppermute(value, axis, pairs)


def rope_angles(position_ids):
    pieces = []
    for axis_number, extent in enumerate((HSIZE // 8, 7 * HSIZE // 16, 7 * HSIZE // 16)):
        freq = jnp.power(
            jnp.float32(10000.0), -2.0 * jnp.arange(extent // 2, dtype=jnp.float32) / extent
        )
        pieces.append(position_ids[axis_number].astype(jnp.float32)[:, None] * freq[None, :])
    return jnp.concatenate(pieces, axis=1)


def rotate(values, angle):
    half_width = values.shape[-1] // 2
    first = values[..., :half_width]
    second = values[..., half_width:]
    cosine = jnp.cos(angle)
    sine = jnp.sin(angle)
    return jnp.concatenate(
        [first * cosine - second * sine, first * sine + second * cosine], axis=-1
    )


def attend_kernel(lens_ref, q_ref, k_ref, v_ref, kt_ref, vt_ref, o_ref, s_scr, acc_scr, l_scr):
    member = pl.program_id(0)
    length = lens_ref[member]
    factor = HSIZE ** (-0.5)
    q = q_ref[...]
    rows = q.shape[0]
    n_keys = k_ref.shape[0]
    n_chunks = n_keys // KBLOCK
    dims = (((1,), (1,)), ((), ()))

    def scores(c, top):
        start = pl.multiple_of(c * KBLOCK, KBLOCK)
        s = lax.dot_general(q, k_ref[pl.ds(start, KBLOCK), :], dims,
                            preferred_element_type=jnp.float32) * factor
        s_scr[:, pl.ds(start, KBLOCK)] = s
        return jnp.maximum(top, jnp.max(s, axis=1, keepdims=True))

    top = lax.fori_loop(0, n_chunks, scores,
                        jnp.full((rows, 1), -jnp.inf, jnp.float32))
    st = lax.dot_general(q, kt_ref[...], dims, preferred_element_type=jnp.float32) * factor
    live = lax.broadcasted_iota(jnp.int32, st.shape, 1) < length
    st = jnp.where(live, st, jnp.float32(-1e30))
    top = jnp.maximum(top, jnp.max(st, axis=1, keepdims=True))
    pt = jnp.where(live, jnp.exp(st - top), jnp.float32(0.0))
    l_scr[...] = jnp.sum(pt, axis=1, keepdims=True)
    acc_scr[...] = jnp.dot(pt.astype(jnp.bfloat16), vt_ref[...],
                           preferred_element_type=jnp.float32)

    def weigh(c, carry):
        start = pl.multiple_of(c * KBLOCK, KBLOCK)
        p = jnp.exp(s_scr[:, pl.ds(start, KBLOCK)] - top)
        l_scr[...] += jnp.sum(p, axis=1, keepdims=True)
        acc_scr[...] += jnp.dot(p.astype(jnp.bfloat16), v_ref[pl.ds(start, KBLOCK), :],
                                preferred_element_type=jnp.float32)
        return carry

    lax.fori_loop(0, n_chunks, weigh, 0)
    o_ref[...] = (acc_scr[...] / l_scr[...]).astype(o_ref.dtype)


def attend_members(qkv, text_kv, lengths):
    members, img = qkv.shape[1], qkv.shape[2]
    txt = text_kv.shape[2]
    nq = img // QBLOCK
    grid_spec = pltpu.PrefetchScalarGridSpec(
        num_scalar_prefetch=1,
        grid=(members, nq),
        in_specs=[
            pl.BlockSpec((None, None, QBLOCK, HSIZE), lambda m, i, lens: (0, m, i, 0)),
            pl.BlockSpec((None, None, img, HSIZE), lambda m, i, lens: (1, m, 0, 0)),
            pl.BlockSpec((None, None, img, HSIZE), lambda m, i, lens: (2, m, 0, 0)),
            pl.BlockSpec((None, None, txt, HSIZE), lambda m, i, lens: (0, m, 0, 0)),
            pl.BlockSpec((None, None, txt, HSIZE), lambda m, i, lens: (1, m, 0, 0)),
        ],
        out_specs=pl.BlockSpec((None, QBLOCK, HSIZE), lambda m, i, lens: (m, i, 0)),
        scratch_shapes=[
            pltpu.VMEM((QBLOCK, img), jnp.float32),
            pltpu.VMEM((QBLOCK, HSIZE), jnp.float32),
            pltpu.VMEM((QBLOCK, 1), jnp.float32),
        ],
    )
    flops = members * img * (img + txt) * HSIZE * 4
    return pl.pallas_call(
        attend_kernel,
        grid_spec=grid_spec,
        out_shape=jax.ShapeDtypeStruct((members, img, HSIZE), jnp.bfloat16),
        compiler_params=pltpu.CompilerParams(
            dimension_semantics=("arbitrary", "arbitrary"),
            vmem_limit_bytes=48 * 1024 * 1024,
        ),
        cost_estimate=pl.CostEstimate(
            flops=flops,
            transcendentals=members * img * (img + txt),
            bytes_accessed=members * (img * 4 + txt * 2) * HSIZE * 2,
        ),
    )(lengths, qkv, qkv, qkv, text_kv, text_kv)


def roster(fraction):
    return 3.0 * fraction / (1.0 + 2.0 * fraction)


def shards(
    latents,
    hidden_img,
    query_img,
    key_img,
    value_img,
    key_txt,
    value_txt,
    text_len,
    img_ids,
    t_index,
    g_index,
    proj_weight,
    attn_gate,
    final_shift,
    final_scale,
    out_weight,
    out_bias,
):
    img_rows = query_img.shape[1]
    prompt_count = query_img.shape[2]
    feature_width = query_img.shape[3]
    head_count = feature_width // HSIZE
    text_rows = key_txt.shape[1]
    members = prompt_count * head_count
    groups = lax.axis_size("seq")
    held = members // groups
    angle = rope_angles(img_ids)[:, None, :]
    rot_query = rotate(
        query_img[0].reshape(img_rows, members, HSIZE).astype(jnp.float32), angle
    ).astype(jnp.bfloat16)
    rot_key = rotate(
        key_img[0].reshape(img_rows, members, HSIZE).astype(jnp.float32), angle
    ).astype(jnp.bfloat16)
    vals = value_img[0].reshape(img_rows, members, HSIZE)
    stacked = jnp.stack([rot_query, rot_key, vals])
    stacked = stacked.reshape(3, img_rows, groups, held, HSIZE).transpose(2, 0, 3, 1, 4)
    text_stacked = jnp.stack(
        [key_txt[0].reshape(text_rows, members, HSIZE), value_txt[0].reshape(text_rows, members, HSIZE)]
    )
    text_stacked = text_stacked.reshape(2, text_rows, groups, held, HSIZE).transpose(2, 0, 3, 1, 4)
    got = lax.all_to_all(stacked, "seq", 0, 0, tiled=True)
    got_text = lax.all_to_all(text_stacked, "seq", 0, 0, tiled=True)
    got = got.reshape(groups, 3, held, img_rows, HSIZE).transpose(1, 2, 0, 3, 4)
    got = got.reshape(3, held, groups * img_rows, HSIZE)
    got_text = got_text.reshape(groups, 2, held, text_rows, HSIZE).transpose(1, 2, 0, 3, 4)
    got_text = got_text.reshape(2, held, groups * text_rows, HSIZE)
    first_member = lax.axis_index("seq") * held
    member_ids = first_member + jnp.arange(held, dtype=jnp.int32)
    lengths = jnp.take(text_len[0], member_ids // head_count)
    attended = attend_members(got, got_text, lengths)
    attended = attended.reshape(held, groups, img_rows, HSIZE).transpose(1, 0, 2, 3)
    returned = lax.all_to_all(attended, "seq", 0, 0, tiled=True)
    returned = returned.reshape(members, img_rows, HSIZE).transpose(1, 0, 2)
    flat_attended = returned.reshape(img_rows * prompt_count, feature_width)
    projected = jnp.dot(
        flat_attended,
        lax.all_gather(proj_weight, ("cfg", "seq"), axis=0, tiled=True),
        preferred_element_type=jnp.float32,
    )
    projected = projected.reshape(img_rows, prompt_count, hidden_img.shape[3])
    residual = hidden_img[0].astype(jnp.float32) + attn_gate[0][None] * projected
    mean_value = jnp.mean(residual, axis=-1, keepdims=True)
    centred = residual - mean_value
    spread = jnp.mean(centred * centred, axis=-1, keepdims=True)
    normed = centred * lax.rsqrt(spread + 1e-06)
    modulated = (normed * (1.0 + final_scale[0][None]) + final_shift[0][None]).astype(jnp.bfloat16)
    velocity = (
        jnp.dot(
            modulated.reshape(img_rows * prompt_count, hidden_img.shape[3]),
            out_weight,
            preferred_element_type=jnp.float32,
        )
        + out_bias[None, :]
    )
    velocity = velocity.reshape(img_rows, prompt_count, out_weight.shape[1])
    kept = latents.shape[2]
    strength = (1.0 + 0.5 * g_index.astype(jnp.float32))[None, :, None]
    partner = partner_2(velocity, "cfg", 0)
    own_half = lax.axis_index("cfg")
    cond_full = jnp.where(own_half == 0, velocity, partner)
    uncond_full = jnp.where(own_half == 0, partner, velocity)
    guided_full = uncond_full + strength * (cond_full - uncond_full)
    guided = lax.dynamic_slice_in_dim(guided_full, own_half * kept, kept, 2)
    moment = t_index.astype(jnp.float32)
    sigma_now = roster(moment / STEPS)[None, :, None]
    sigma_next = roster((moment - 1.0) / STEPS)[None, :, None]
    next_latents = latents + (sigma_next - sigma_now) * guided
    denoised = latents - sigma_now * guided
    return (next_latents, denoised)


def solution(mesh):
    placed = (
        P("seq", "req", "cfg"),
        P("cfg", "seq", "req", None),
        P("cfg", "seq", "req", None),
        P("cfg", "seq", "req", None),
        P("cfg", "seq", "req", None),
        P("cfg", "seq", "req", None),
        P("cfg", "seq", "req", None),
        P("cfg", "req"),
        P(None, "seq"),
        P("req"),
        P("req"),
        P(("cfg", "seq"), None),
        P("cfg", "req", None),
        P("cfg", "req", None),
        P("cfg", "req", None),
        P(),
        P(),
    )
    return jax.shard_map(
        shards,
        mesh=mesh,
        in_specs=placed,
        out_specs=(P("seq", "req", "cfg"), P("seq", "req", "cfg")),
        check_vma=False,
    )
```

```python
import math

import jax
import jax.numpy as jnp
from jax import lax
from jax.experimental import pallas as pl
from jax.experimental.pallas import tpu as pltpu
from jax.sharding import PartitionSpec as P

HSIZE = 128
STEPS = 28
QBLOCK = 512
KBLOCK = 512


def partner_2(value, axis, distance):
    mask = 2**distance
    pairs = [(source, source ^ mask) for source in range(lax.axis_size(axis))]
    return lax.ppermute(value, axis, pairs)


def rope_angles(position_ids):
    pieces = []
    for axis_number, extent in enumerate((HSIZE // 8, 7 * HSIZE // 16, 7 * HSIZE // 16)):
        freq = jnp.power(
            jnp.float32(10000.0), -2.0 * jnp.arange(extent // 2, dtype=jnp.float32) / extent
        )
        pieces.append(position_ids[axis_number].astype(jnp.float32)[:, None] * freq[None, :])
    return jnp.concatenate(pieces, axis=1)


def rotate(values, angle):
    half_width = values.shape[-1] // 2
    first = values[..., :half_width]
    second = values[..., half_width:]
    cosine = jnp.cos(angle)
    sine = jnp.sin(angle)
    return jnp.concatenate(
        [first * cosine - second * sine, first * sine + second * cosine], axis=-1
    )


def attend_kernel(len_ref, q_ref, k_ref, v_ref, kt_ref, vt_ref, o_ref, s_scr, m_scr, l_scr, acc_scr):
    length = len_ref[0]
    scale = (HSIZE ** (-0.5)) * math.log2(math.e)
    rows = QBLOCK
    per_chunk = KBLOCK // k_ref.shape[1]
    n_chunks = k_ref.shape[0] // per_chunk
    lanes = 128
    dims = (((1,), (1,)), ((), ()))
    q = q_ref[...].reshape(rows, HSIZE)
    m_scr[...] = jnp.full((rows, lanes), -jnp.inf, jnp.float32)

    def scores(c, carry):
        start = pl.multiple_of(c * KBLOCK, KBLOCK)
        keys = k_ref[pl.ds(c * per_chunk, per_chunk)].reshape(KBLOCK, HSIZE)
        s = lax.dot_general(q, keys, dims, preferred_element_type=jnp.float32) * scale
        s_scr[:, pl.ds(start, KBLOCK)] = s
        top = m_scr[...]
        for j in range(KBLOCK // lanes):
            top = jnp.maximum(top, s[:, j * lanes:(j + 1) * lanes])
        m_scr[...] = top
        return carry

    lax.fori_loop(0, n_chunks, scores, 0)
    text_keys = kt_ref[...].reshape(-1, HSIZE)
    st = lax.dot_general(q, text_keys, dims, preferred_element_type=jnp.float32) * scale
    live = lax.broadcasted_iota(jnp.int32, st.shape, 1) < length
    st = jnp.where(live, st, jnp.float32(-1e30))
    top = m_scr[...]
    for j in range(st.shape[1] // lanes):
        top = jnp.maximum(top, st[:, j * lanes:(j + 1) * lanes])
    top = jnp.max(top, axis=1, keepdims=True)
    m_scr[...] = jnp.broadcast_to(top, (rows, lanes))
    pt = jnp.where(live, jnp.exp2(st - top), jnp.float32(0.0))
    total = pt[:, 0:lanes]
    for j in range(1, st.shape[1] // lanes):
        total = total + pt[:, j * lanes:(j + 1) * lanes]
    l_scr[...] = total
    acc_scr[...] = jnp.dot(pt.astype(jnp.bfloat16), vt_ref[...].reshape(-1, HSIZE),
                           preferred_element_type=jnp.float32)

    def weigh(c, carry):
        start = pl.multiple_of(c * KBLOCK, KBLOCK)
        tb = m_scr[...]
        parts = [jnp.exp2(s_scr[:, pl.ds(start + j * lanes, lanes)] - tb)
                 for j in range(KBLOCK // lanes)]
        total = l_scr[...]
        for part in parts:
            total = total + part
        l_scr[...] = total
        p = jnp.concatenate(parts, axis=1).astype(jnp.bfloat16)
        vals = v_ref[pl.ds(c * per_chunk, per_chunk)].reshape(KBLOCK, HSIZE)
        acc_scr[...] += jnp.dot(p, vals, preferred_element_type=jnp.float32)
        return carry

    lax.fori_loop(0, n_chunks, weigh, 0)
    denom = jnp.sum(l_scr[...], axis=1, keepdims=True)
    o_ref[...] = (acc_scr[...] / denom).astype(o_ref.dtype).reshape(o_ref.shape)


def attend_member(chunk, text_chunk, length):
    sources, tokens = chunk.shape[0], chunk.shape[2]
    text_tokens = text_chunk.shape[2]
    img = sources * tokens
    txt = sources * text_tokens
    per_block = QBLOCK // tokens
    grid_spec = pltpu.PrefetchScalarGridSpec(
        num_scalar_prefetch=1,
        grid=(img // QBLOCK,),
        in_specs=[
            pl.BlockSpec((per_block, None, tokens, HSIZE), lambda i, lens: (i, 0, 0, 0)),
            pl.BlockSpec((sources, None, tokens, HSIZE), lambda i, lens: (0, 1, 0, 0)),
            pl.BlockSpec((sources, None, tokens, HSIZE), lambda i, lens: (0, 2, 0, 0)),
            pl.BlockSpec((sources, None, text_tokens, HSIZE), lambda i, lens: (0, 0, 0, 0)),
            pl.BlockSpec((sources, None, text_tokens, HSIZE), lambda i, lens: (0, 1, 0, 0)),
        ],
        out_specs=pl.BlockSpec((per_block, tokens, HSIZE), lambda i, lens: (i, 0, 0)),
        scratch_shapes=[
            pltpu.VMEM((QBLOCK, img), jnp.float32),
            pltpu.VMEM((QBLOCK, 128), jnp.float32),
            pltpu.VMEM((QBLOCK, 128), jnp.float32),
            pltpu.VMEM((QBLOCK, HSIZE), jnp.float32),
        ],
    )
    return pl.pallas_call(
        attend_kernel,
        grid_spec=grid_spec,
        out_shape=jax.ShapeDtypeStruct((sources, tokens, HSIZE), jnp.bfloat16),
        compiler_params=pltpu.CompilerParams(
            dimension_semantics=("arbitrary",),
            vmem_limit_bytes=48 * 1024 * 1024,
        ),
        cost_estimate=pl.CostEstimate(
            flops=img * (img + txt) * HSIZE * 4,
            transcendentals=img * (img + txt),
            bytes_accessed=(img * 4 + txt * 2) * HSIZE * 2,
        ),
    )(length, chunk, chunk, chunk, text_chunk, text_chunk)


def roster(fraction):
    return 3.0 * fraction / (1.0 + 2.0 * fraction)


def shards(
    latents,
    hidden_img,
    query_img,
    key_img,
    value_img,
    key_txt,
    value_txt,
    text_len,
    img_ids,
    t_index,
    g_index,
    proj_weight,
    attn_gate,
    final_shift,
    final_scale,
    out_weight,
    out_bias,
):
    img_rows = query_img.shape[1]
    prompt_count = query_img.shape[2]
    feature_width = query_img.shape[3]
    head_count = feature_width // HSIZE
    text_rows = key_txt.shape[1]
    members = prompt_count * head_count
    groups = lax.axis_size("seq")
    held = members // groups
    angle = rope_angles(img_ids)[:, None, :]
    rot_query = rotate(
        query_img[0].reshape(img_rows, members, HSIZE).astype(jnp.float32), angle
    ).astype(jnp.bfloat16)
    rot_key = rotate(
        key_img[0].reshape(img_rows, members, HSIZE).astype(jnp.float32), angle
    ).astype(jnp.bfloat16)
    vals = value_img[0].reshape(img_rows, members, HSIZE)
    stacked = jnp.stack([rot_query, rot_key, vals])
    stacked = stacked.reshape(3, img_rows, groups, held, HSIZE).transpose(2, 0, 3, 1, 4)
    text_stacked = jnp.stack(
        [key_txt[0].reshape(text_rows, members, HSIZE), value_txt[0].reshape(text_rows, members, HSIZE)]
    )
    text_stacked = text_stacked.reshape(2, text_rows, groups, held, HSIZE).transpose(2, 0, 3, 1, 4)
    first_member = lax.axis_index("seq") * held
    returned = []
    for member in range(held):
        got = lax.all_to_all(stacked[:, :, member], "seq", 0, 0, tiled=True)
        got_text = lax.all_to_all(text_stacked[:, :, member], "seq", 0, 0, tiled=True)
        prompt_of = (first_member + member) // head_count
        length = jnp.take(text_len[0], prompt_of)[None]
        attended = attend_member(got, got_text, length)
        returned.append(lax.all_to_all(attended, "seq", 0, 0, tiled=True))
    returned = jnp.stack(returned, axis=1).reshape(members, img_rows, HSIZE).transpose(1, 0, 2)
    flat_attended = returned.reshape(img_rows * prompt_count, feature_width)
    projected = jnp.dot(
        flat_attended,
        lax.all_gather(proj_weight, ("cfg", "seq"), axis=0, tiled=True),
        preferred_element_type=jnp.float32,
    )
    projected = projected.reshape(img_rows, prompt_count, hidden_img.shape[3])
    residual = hidden_img[0].astype(jnp.float32) + attn_gate[0][None] * projected
    mean_value = jnp.mean(residual, axis=-1, keepdims=True)
    centred = residual - mean_value
    spread = jnp.mean(centred * centred, axis=-1, keepdims=True)
    normed = centred * lax.rsqrt(spread + 1e-06)
    modulated = (normed * (1.0 + final_scale[0][None]) + final_shift[0][None]).astype(jnp.bfloat16)
    velocity = (
        jnp.dot(
            modulated.reshape(img_rows * prompt_count, hidden_img.shape[3]),
            out_weight,
            preferred_element_type=jnp.float32,
        )
        + out_bias[None, :]
    )
    velocity = velocity.reshape(img_rows, prompt_count, out_weight.shape[1])
    kept = latents.shape[2]
    strength = (1.0 + 0.5 * g_index.astype(jnp.float32))[None, :, None]
    partner = partner_2(velocity, "cfg", 0)
    own_half = lax.axis_index("cfg")
    cond_full = jnp.where(own_half == 0, velocity, partner)
    uncond_full = jnp.where(own_half == 0, partner, velocity)
    guided_full = uncond_full + strength * (cond_full - uncond_full)
    guided = lax.dynamic_slice_in_dim(guided_full, own_half * kept, kept, 2)
    moment = t_index.astype(jnp.float32)
    sigma_now = roster(moment / STEPS)[None, :, None]
    sigma_next = roster((moment - 1.0) / STEPS)[None, :, None]
    next_latents = latents + (sigma_next - sigma_now) * guided
    denoised = latents - sigma_now * guided
    return (next_latents, denoised)


def solution(mesh):
    placed = (
        P("seq", "req", "cfg"),
        P("cfg", "seq", "req", None),
        P("cfg", "seq", "req", None),
        P("cfg", "seq", "req", None),
        P("cfg", "seq", "req", None),
        P("cfg", "seq", "req", None),
        P("cfg", "seq", "req", None),
        P("cfg", "req"),
        P(None, "seq"),
        P("req"),
        P("req"),
        P(("cfg", "seq"), None),
        P("cfg", "req", None),
        P("cfg", "req", None),
        P("cfg", "req", None),
        P(),
        P(),
    )
    return jax.shard_map(
        shards,
        mesh=mesh,
        in_specs=placed,
        out_specs=(P("seq", "req", "cfg"), P("seq", "req", "cfg")),
        check_vma=False,
    )
```

```python
import math

import jax
import jax.numpy as jnp
from jax import lax
from jax.experimental import pallas as pl
from jax.experimental.pallas import tpu as pltpu
from jax.sharding import PartitionSpec as P

HSIZE = 128
STEPS = 28
QBLOCK = 512
KBLOCK = 512


def partner_2(value, axis, distance):
    mask = 2**distance
    pairs = [(source, source ^ mask) for source in range(lax.axis_size(axis))]
    return lax.ppermute(value, axis, pairs)


def rope_angles(position_ids):
    pieces = []
    for axis_number, extent in enumerate((HSIZE // 8, 7 * HSIZE // 16, 7 * HSIZE // 16)):
        freq = jnp.power(
            jnp.float32(10000.0), -2.0 * jnp.arange(extent // 2, dtype=jnp.float32) / extent
        )
        pieces.append(position_ids[axis_number].astype(jnp.float32)[:, None] * freq[None, :])
    return jnp.concatenate(pieces, axis=1)


def rotate(values, angle):
    half_width = values.shape[-1] // 2
    first = values[..., :half_width]
    second = values[..., half_width:]
    cosine = jnp.cos(angle)
    sine = jnp.sin(angle)
    return jnp.concatenate(
        [first * cosine - second * sine, first * sine + second * cosine], axis=-1
    )


def attend_kernel(len_ref, q_ref, k_ref, v_ref, kt_ref, vt_ref, o_ref, s_scr, m_scr, l_scr, acc_scr):
    length = len_ref[0]
    scale = (HSIZE ** (-0.5)) * math.log2(math.e)
    rows = QBLOCK
    per_chunk = KBLOCK // k_ref.shape[1]
    n_chunks = k_ref.shape[0] // per_chunk
    lanes = 128
    dims = (((1,), (1,)), ((), ()))
    q = q_ref[...].reshape(rows, HSIZE)
    m_scr[...] = jnp.full((rows, lanes), -jnp.inf, jnp.float32)

    def scores(c, carry):
        start = pl.multiple_of(c * KBLOCK, KBLOCK)
        keys = k_ref[pl.ds(c * per_chunk, per_chunk)].reshape(KBLOCK, HSIZE)
        s = lax.dot_general(q, keys, dims, preferred_element_type=jnp.float32) * scale
        s_scr[:, pl.ds(start, KBLOCK)] = s
        top = m_scr[...]
        for j in range(KBLOCK // lanes):
            top = jnp.maximum(top, s[:, j * lanes:(j + 1) * lanes])
        m_scr[...] = top
        return carry

    lax.fori_loop(0, n_chunks, scores, 0)
    text_keys = kt_ref[...].reshape(-1, HSIZE)
    st = lax.dot_general(q, text_keys, dims, preferred_element_type=jnp.float32) * scale
    live = lax.broadcasted_iota(jnp.int32, st.shape, 1) < length
    st = jnp.where(live, st, jnp.float32(-1e30))
    top = m_scr[...]
    for j in range(st.shape[1] // lanes):
        top = jnp.maximum(top, st[:, j * lanes:(j + 1) * lanes])
    top = jnp.max(top, axis=1, keepdims=True)
    m_scr[...] = jnp.broadcast_to(top, (rows, lanes))
    pt = jnp.where(live, jnp.exp2(st - top), jnp.float32(0.0))
    total = pt[:, 0:lanes]
    for j in range(1, st.shape[1] // lanes):
        total = total + pt[:, j * lanes:(j + 1) * lanes]
    l_scr[...] = total
    acc_scr[...] = jnp.dot(pt.astype(jnp.bfloat16), vt_ref[...].reshape(-1, HSIZE),
                           preferred_element_type=jnp.float32)

    def weigh(c, carry):
        start = pl.multiple_of(c * KBLOCK, KBLOCK)
        tb = m_scr[...]
        parts = [jnp.exp2(s_scr[:, pl.ds(start + j * lanes, lanes)] - tb)
                 for j in range(KBLOCK // lanes)]
        total = l_scr[...]
        for part in parts:
            total = total + part
        l_scr[...] = total
        p = jnp.concatenate(parts, axis=1).astype(jnp.bfloat16)
        vals = v_ref[pl.ds(c * per_chunk, per_chunk)].reshape(KBLOCK, HSIZE)
        acc_scr[...] += jnp.dot(p, vals, preferred_element_type=jnp.float32)
        return carry

    lax.fori_loop(0, n_chunks, weigh, 0)
    denom = jnp.sum(l_scr[...], axis=1, keepdims=True)
    o_ref[...] = (acc_scr[...] / denom).astype(o_ref.dtype).reshape(o_ref.shape)


def attend_member(chunk, text_chunk, length):
    sources, tokens = chunk.shape[0], chunk.shape[2]
    text_tokens = text_chunk.shape[2]
    img = sources * tokens
    txt = sources * text_tokens
    per_block = QBLOCK // tokens
    grid_spec = pltpu.PrefetchScalarGridSpec(
        num_scalar_prefetch=1,
        grid=(img // QBLOCK,),
        in_specs=[
            pl.BlockSpec((per_block, None, tokens, HSIZE), lambda i, lens: (i, 0, 0, 0)),
            pl.BlockSpec((sources, None, tokens, HSIZE), lambda i, lens: (0, 1, 0, 0)),
            pl.BlockSpec((sources, None, tokens, HSIZE), lambda i, lens: (0, 2, 0, 0)),
            pl.BlockSpec((sources, None, text_tokens, HSIZE), lambda i, lens: (0, 0, 0, 0)),
            pl.BlockSpec((sources, None, text_tokens, HSIZE), lambda i, lens: (0, 1, 0, 0)),
        ],
        out_specs=pl.BlockSpec((per_block, tokens, HSIZE), lambda i, lens: (i, 0, 0)),
        scratch_shapes=[
            pltpu.VMEM((QBLOCK, img), jnp.float32),
            pltpu.VMEM((QBLOCK, 128), jnp.float32),
            pltpu.VMEM((QBLOCK, 128), jnp.float32),
            pltpu.VMEM((QBLOCK, HSIZE), jnp.float32),
        ],
    )
    return pl.pallas_call(
        attend_kernel,
        grid_spec=grid_spec,
        out_shape=jax.ShapeDtypeStruct((sources, tokens, HSIZE), jnp.bfloat16),
        compiler_params=pltpu.CompilerParams(
            dimension_semantics=("arbitrary",),
            vmem_limit_bytes=48 * 1024 * 1024,
        ),
        cost_estimate=pl.CostEstimate(
            flops=img * (img + txt) * HSIZE * 4,
            transcendentals=img * (img + txt),
            bytes_accessed=(img * 4 + txt * 2) * HSIZE * 2,
        ),
    )(length, chunk, chunk, chunk, text_chunk, text_chunk)


def prep_kernel(cs_ref, q_ref, k_ref, v_ref, kt_ref, vt_ref, o_ref, ot_ref):
    cosine = cs_ref[0]
    sine = cs_ref[1]
    prompts = q_ref.shape[1]
    heads = q_ref.shape[2] // HSIZE
    held = o_ref.shape[0]
    per_prompt = heads // held
    def one_head(h, carry):
        cols = pl.ds(pl.multiple_of(h * HSIZE, HSIZE), HSIZE)
        member = h % held
        for p in range(prompts):
            dest = p * per_prompt + h // held
            for t, ref in enumerate((q_ref, k_ref)):
                x = ref[:, p, cols].astype(jnp.float32)
                turned = pltpu.roll(x, HSIZE // 2, 1)
                o_ref[member, dest, t] = (x * cosine + turned * sine).astype(o_ref.dtype)
            o_ref[member, dest, 2] = v_ref[:, p, cols]
            ot_ref[member, dest, 0] = kt_ref[:, p, cols]
            ot_ref[member, dest, 1] = vt_ref[:, p, cols]
        return carry

    lax.fori_loop(0, heads, one_head, 0)


def prep_send(cs, q, k, v, kt, vt, groups):
    tokens, prompts, width = q.shape
    text_tokens = kt.shape[0]
    held = prompts * (width // HSIZE) // groups
    vmem = pl.BlockSpec(memory_space=pltpu.VMEM)
    return pl.pallas_call(
        prep_kernel,
        in_specs=[vmem] * 6,
        out_specs=[vmem, vmem],
        out_shape=[
            jax.ShapeDtypeStruct((held, groups, 3, tokens, HSIZE), jnp.bfloat16),
            jax.ShapeDtypeStruct((held, groups, 2, text_tokens, HSIZE), jnp.bfloat16),
        ],
        compiler_params=pltpu.CompilerParams(vmem_limit_bytes=48 * 1024 * 1024),
        cost_estimate=pl.CostEstimate(
            flops=tokens * prompts * width * 12,
            transcendentals=0,
            bytes_accessed=(tokens * 3 + text_tokens * 2) * prompts * width * 4,
        ),
    )(cs, q, k, v, kt, vt)


def roster(fraction):
    return 3.0 * fraction / (1.0 + 2.0 * fraction)


def shards(
    latents,
    hidden_img,
    query_img,
    key_img,
    value_img,
    key_txt,
    value_txt,
    text_len,
    img_ids,
    t_index,
    g_index,
    proj_weight,
    attn_gate,
    final_shift,
    final_scale,
    out_weight,
    out_bias,
):
    img_rows = query_img.shape[1]
    prompt_count = query_img.shape[2]
    feature_width = query_img.shape[3]
    head_count = feature_width // HSIZE
    text_rows = key_txt.shape[1]
    members = prompt_count * head_count
    groups = lax.axis_size("seq")
    held = members // groups
    angle = rope_angles(img_ids)
    cosine = jnp.cos(angle)
    sine = jnp.sin(angle)
    cs = jnp.stack([
        jnp.concatenate([cosine, cosine], axis=1),
        jnp.concatenate([-sine, sine], axis=1),
    ])
    stacked, text_stacked = prep_send(
        cs, query_img[0], key_img[0], value_img[0], key_txt[0], value_txt[0], groups
    )
    first_member = lax.axis_index("seq") * held
    returned = []
    for member in range(held):
        got = lax.all_to_all(stacked[member], "seq", 0, 0, tiled=True)
        got_text = lax.all_to_all(text_stacked[member], "seq", 0, 0, tiled=True)
        prompt_of = (first_member + member) // head_count
        length = jnp.take(text_len[0], prompt_of)[None]
        attended = attend_member(got, got_text, length)
        returned.append(lax.all_to_all(attended, "seq", 0, 0, tiled=True))
    returned = jnp.stack(returned, axis=1).reshape(members, img_rows, HSIZE).transpose(1, 0, 2)
    flat_attended = returned.reshape(img_rows * prompt_count, feature_width)
    projected = jnp.dot(
        flat_attended,
        lax.all_gather(proj_weight, ("cfg", "seq"), axis=0, tiled=True),
        preferred_element_type=jnp.float32,
    )
    projected = projected.reshape(img_rows, prompt_count, hidden_img.shape[3])
    residual = hidden_img[0].astype(jnp.float32) + attn_gate[0][None] * projected
    mean_value = jnp.mean(residual, axis=-1, keepdims=True)
    centred = residual - mean_value
    spread = jnp.mean(centred * centred, axis=-1, keepdims=True)
    normed = centred * lax.rsqrt(spread + 1e-06)
    modulated = (normed * (1.0 + final_scale[0][None]) + final_shift[0][None]).astype(jnp.bfloat16)
    velocity = (
        jnp.dot(
            modulated.reshape(img_rows * prompt_count, hidden_img.shape[3]),
            out_weight,
            preferred_element_type=jnp.float32,
        )
        + out_bias[None, :]
    )
    velocity = velocity.reshape(img_rows, prompt_count, out_weight.shape[1])
    kept = latents.shape[2]
    strength = (1.0 + 0.5 * g_index.astype(jnp.float32))[None, :, None]
    partner = partner_2(velocity, "cfg", 0)
    own_half = lax.axis_index("cfg")
    cond_full = jnp.where(own_half == 0, velocity, partner)
    uncond_full = jnp.where(own_half == 0, partner, velocity)
    guided_full = uncond_full + strength * (cond_full - uncond_full)
    guided = lax.dynamic_slice_in_dim(guided_full, own_half * kept, kept, 2)
    moment = t_index.astype(jnp.float32)
    sigma_now = roster(moment / STEPS)[None, :, None]
    sigma_next = roster((moment - 1.0) / STEPS)[None, :, None]
    next_latents = latents + (sigma_next - sigma_now) * guided
    denoised = latents - sigma_now * guided
    return (next_latents, denoised)


def solution(mesh):
    placed = (
        P("seq", "req", "cfg"),
        P("cfg", "seq", "req", None),
        P("cfg", "seq", "req", None),
        P("cfg", "seq", "req", None),
        P("cfg", "seq", "req", None),
        P("cfg", "seq", "req", None),
        P("cfg", "seq", "req", None),
        P("cfg", "req"),
        P(None, "seq"),
        P("req"),
        P("req"),
        P(("cfg", "seq"), None),
        P("cfg", "req", None),
        P("cfg", "req", None),
        P("cfg", "req", None),
        P(),
        P(),
    )
    return jax.shard_map(
        shards,
        mesh=mesh,
        in_specs=placed,
        out_specs=(P("seq", "req", "cfg"), P("seq", "req", "cfg")),
        check_vma=False,
    )
```

```python
import math

import jax
import jax.numpy as jnp
from jax import lax
from jax.experimental import pallas as pl
from jax.experimental.pallas import tpu as pltpu
from jax.sharding import PartitionSpec as P

HSIZE = 128
STEPS = 28
QBLOCK = 512
KBLOCK = 512


def partner_2(value, axis, distance):
    mask = 2**distance
    pairs = [(source, source ^ mask) for source in range(lax.axis_size(axis))]
    return lax.ppermute(value, axis, pairs)


def rope_angles(position_ids):
    pieces = []
    for axis_number, extent in enumerate((HSIZE // 8, 7 * HSIZE // 16, 7 * HSIZE // 16)):
        freq = jnp.power(
            jnp.float32(10000.0), -2.0 * jnp.arange(extent // 2, dtype=jnp.float32) / extent
        )
        pieces.append(position_ids[axis_number].astype(jnp.float32)[:, None] * freq[None, :])
    return jnp.concatenate(pieces, axis=1)


def rotate(values, angle):
    half_width = values.shape[-1] // 2
    first = values[..., :half_width]
    second = values[..., half_width:]
    cosine = jnp.cos(angle)
    sine = jnp.sin(angle)
    return jnp.concatenate(
        [first * cosine - second * sine, first * sine + second * cosine], axis=-1
    )


def attend_kernel(len_ref, q_ref, k_ref, v_ref, kt_ref, vt_ref, o_ref, s_scr, m_scr, l_scr, acc_scr):
    length = len_ref[0]
    scale = (HSIZE ** (-0.5)) * math.log2(math.e)
    rows = QBLOCK
    per_chunk = KBLOCK // k_ref.shape[1]
    n_chunks = k_ref.shape[0] // per_chunk
    lanes = 128
    dims = (((1,), (1,)), ((), ()))
    q = q_ref[...].reshape(rows, HSIZE)
    m_scr[...] = jnp.full((rows, lanes), -jnp.inf, jnp.float32)

    def scores(c, carry):
        start = pl.multiple_of(c * KBLOCK, KBLOCK)
        keys = k_ref[pl.ds(c * per_chunk, per_chunk)].reshape(KBLOCK, HSIZE)
        s = lax.dot_general(q, keys, dims, preferred_element_type=jnp.float32) * scale
        s_scr[:, pl.ds(start, KBLOCK)] = s
        top = m_scr[...]
        for j in range(KBLOCK // lanes):
            top = jnp.maximum(top, s[:, j * lanes:(j + 1) * lanes])
        m_scr[...] = top
        return carry

    lax.fori_loop(0, n_chunks, scores, 0)
    text_keys = kt_ref[...].reshape(-1, HSIZE)
    st = lax.dot_general(q, text_keys, dims, preferred_element_type=jnp.float32) * scale
    live = lax.broadcasted_iota(jnp.int32, st.shape, 1) < length
    st = jnp.where(live, st, jnp.float32(-1e30))
    top = m_scr[...]
    for j in range(st.shape[1] // lanes):
        top = jnp.maximum(top, st[:, j * lanes:(j + 1) * lanes])
    top = jnp.max(top, axis=1, keepdims=True)
    m_scr[...] = jnp.broadcast_to(top, (rows, lanes))
    pt = jnp.where(live, jnp.exp2(st - top), jnp.float32(0.0))
    total = pt[:, 0:lanes]
    for j in range(1, st.shape[1] // lanes):
        total = total + pt[:, j * lanes:(j + 1) * lanes]
    l_scr[...] = total
    acc_scr[...] = jnp.dot(pt.astype(jnp.bfloat16), vt_ref[...].reshape(-1, HSIZE),
                           preferred_element_type=jnp.float32)

    def weigh(c, carry):
        start = pl.multiple_of(c * KBLOCK, KBLOCK)
        tb = m_scr[...]
        parts = [jnp.exp2(s_scr[:, pl.ds(start + j * lanes, lanes)] - tb)
                 for j in range(KBLOCK // lanes)]
        total = l_scr[...]
        for part in parts:
            total = total + part
        l_scr[...] = total
        p = jnp.concatenate(parts, axis=1).astype(jnp.bfloat16)
        vals = v_ref[pl.ds(c * per_chunk, per_chunk)].reshape(KBLOCK, HSIZE)
        acc_scr[...] += jnp.dot(p, vals, preferred_element_type=jnp.float32)
        return carry

    lax.fori_loop(0, n_chunks, weigh, 0)
    denom = jnp.sum(l_scr[...], axis=1, keepdims=True)
    o_ref[...] = (acc_scr[...] / denom).astype(o_ref.dtype).reshape(o_ref.shape)


def attend_member(chunk, tokens, text_tokens, length):
    sources = chunk.shape[0]
    img = sources * tokens
    txt = sources * text_tokens
    per_block = QBLOCK // tokens
    text_at = 3 * tokens // text_tokens
    grid_spec = pltpu.PrefetchScalarGridSpec(
        num_scalar_prefetch=1,
        grid=(img // QBLOCK,),
        in_specs=[
            pl.BlockSpec((per_block, tokens, HSIZE), lambda i, lens: (i, 0, 0)),
            pl.BlockSpec((sources, tokens, HSIZE), lambda i, lens: (0, 1, 0)),
            pl.BlockSpec((sources, tokens, HSIZE), lambda i, lens: (0, 2, 0)),
            pl.BlockSpec((sources, text_tokens, HSIZE), lambda i, lens: (0, text_at, 0)),
            pl.BlockSpec((sources, text_tokens, HSIZE), lambda i, lens: (0, text_at + 1, 0)),
        ],
        out_specs=pl.BlockSpec((per_block, tokens, HSIZE), lambda i, lens: (i, 0, 0)),
        scratch_shapes=[
            pltpu.VMEM((QBLOCK, img), jnp.float32),
            pltpu.VMEM((QBLOCK, 128), jnp.float32),
            pltpu.VMEM((QBLOCK, 128), jnp.float32),
            pltpu.VMEM((QBLOCK, HSIZE), jnp.float32),
        ],
    )
    return pl.pallas_call(
        attend_kernel,
        grid_spec=grid_spec,
        out_shape=jax.ShapeDtypeStruct((sources, tokens, HSIZE), jnp.bfloat16),
        compiler_params=pltpu.CompilerParams(
            dimension_semantics=("arbitrary",),
            vmem_limit_bytes=48 * 1024 * 1024,
        ),
        cost_estimate=pl.CostEstimate(
            flops=img * (img + txt) * HSIZE * 4,
            transcendentals=img * (img + txt),
            bytes_accessed=(img * 4 + txt * 2) * HSIZE * 2,
        ),
    )(length, chunk, chunk, chunk, chunk, chunk)


def prep_kernel(cs_ref, q_ref, k_ref, v_ref, kt_ref, vt_ref, *out_refs):
    cosine = cs_ref[0]
    sine = cs_ref[1]
    tokens, prompts = q_ref.shape[0], q_ref.shape[1]
    text_tokens = kt_ref.shape[0]
    heads = q_ref.shape[2] // HSIZE
    held = len(out_refs)
    per_prompt = heads // held
    img_part = 3 * tokens

    def one_pair(hh, carry):
        for member in range(held):
            o_ref = out_refs[member]
            cols = pl.ds(pl.multiple_of((hh * held + member) * HSIZE, HSIZE), HSIZE)
            for p in range(prompts):
                dest = p * per_prompt + hh
                for t, ref in enumerate((q_ref, k_ref)):
                    x = ref[:, p, cols].astype(jnp.float32)
                    turned = pltpu.roll(x, HSIZE // 2, 1)
                    o_ref[dest, t * tokens:(t + 1) * tokens] = (
                        x * cosine + turned * sine).astype(o_ref.dtype)
                o_ref[dest, 2 * tokens:img_part] = v_ref[:, p, cols]
                o_ref[dest, img_part:img_part + text_tokens] = kt_ref[:, p, cols]
                o_ref[dest, img_part + text_tokens:img_part + 2 * text_tokens] = vt_ref[:, p, cols]
        return carry

    lax.fori_loop(0, per_prompt, one_pair, 0)


def prep_send(cs, q, k, v, kt, vt, groups):
    tokens, prompts, width = q.shape
    text_tokens = kt.shape[0]
    held = prompts * (width // HSIZE) // groups
    rows = 3 * tokens + 2 * text_tokens
    vmem = pl.BlockSpec(memory_space=pltpu.VMEM)
    return pl.pallas_call(
        prep_kernel,
        in_specs=[vmem] * 6,
        out_specs=[vmem] * held,
        out_shape=[jax.ShapeDtypeStruct((groups, rows, HSIZE), jnp.bfloat16)] * held,
        compiler_params=pltpu.CompilerParams(vmem_limit_bytes=48 * 1024 * 1024),
        cost_estimate=pl.CostEstimate(
            flops=tokens * prompts * width * 12,
            transcendentals=0,
            bytes_accessed=(tokens * 3 + text_tokens * 2) * prompts * width * 4,
        ),
    )(cs, q, k, v, kt, vt)


def roster(fraction):
    return 3.0 * fraction / (1.0 + 2.0 * fraction)


def shards(
    latents,
    hidden_img,
    query_img,
    key_img,
    value_img,
    key_txt,
    value_txt,
    text_len,
    img_ids,
    t_index,
    g_index,
    proj_weight,
    attn_gate,
    final_shift,
    final_scale,
    out_weight,
    out_bias,
):
    img_rows = query_img.shape[1]
    prompt_count = query_img.shape[2]
    feature_width = query_img.shape[3]
    head_count = feature_width // HSIZE
    text_rows = key_txt.shape[1]
    members = prompt_count * head_count
    groups = lax.axis_size("seq")
    held = members // groups
    angle = rope_angles(img_ids)
    cosine = jnp.cos(angle)
    sine = jnp.sin(angle)
    cs = jnp.stack([
        jnp.concatenate([cosine, cosine], axis=1),
        jnp.concatenate([-sine, sine], axis=1),
    ])
    sends = prep_send(
        cs, query_img[0], key_img[0], value_img[0], key_txt[0], value_txt[0], groups
    )
    first_member = lax.axis_index("seq") * held
    returned = []
    for member in range(held):
        got = lax.all_to_all(sends[member], "seq", 0, 0, tiled=True)
        prompt_of = (first_member + member) // head_count
        length = jnp.take(text_len[0], prompt_of)[None]
        attended = attend_member(got, img_rows, text_rows, length)
        returned.append(lax.all_to_all(attended, "seq", 0, 0, tiled=True))
    returned = jnp.stack(returned, axis=1).reshape(members, img_rows, HSIZE).transpose(1, 0, 2)
    flat_attended = returned.reshape(img_rows * prompt_count, feature_width)
    projected = jnp.dot(
        flat_attended,
        lax.all_gather(proj_weight, ("cfg", "seq"), axis=0, tiled=True),
        preferred_element_type=jnp.float32,
    )
    projected = projected.reshape(img_rows, prompt_count, hidden_img.shape[3])
    residual = hidden_img[0].astype(jnp.float32) + attn_gate[0][None] * projected
    mean_value = jnp.mean(residual, axis=-1, keepdims=True)
    centred = residual - mean_value
    spread = jnp.mean(centred * centred, axis=-1, keepdims=True)
    normed = centred * lax.rsqrt(spread + 1e-06)
    modulated = (normed * (1.0 + final_scale[0][None]) + final_shift[0][None]).astype(jnp.bfloat16)
    velocity = (
        jnp.dot(
            modulated.reshape(img_rows * prompt_count, hidden_img.shape[3]),
            out_weight,
            preferred_element_type=jnp.float32,
        )
        + out_bias[None, :]
    )
    velocity = velocity.reshape(img_rows, prompt_count, out_weight.shape[1])
    kept = latents.shape[2]
    strength = (1.0 + 0.5 * g_index.astype(jnp.float32))[None, :, None]
    partner = partner_2(velocity, "cfg", 0)
    own_half = lax.axis_index("cfg")
    cond_full = jnp.where(own_half == 0, velocity, partner)
    uncond_full = jnp.where(own_half == 0, partner, velocity)
    guided_full = uncond_full + strength * (cond_full - uncond_full)
    guided = lax.dynamic_slice_in_dim(guided_full, own_half * kept, kept, 2)
    moment = t_index.astype(jnp.float32)
    sigma_now = roster(moment / STEPS)[None, :, None]
    sigma_next = roster((moment - 1.0) / STEPS)[None, :, None]
    next_latents = latents + (sigma_next - sigma_now) * guided
    denoised = latents - sigma_now * guided
    return (next_latents, denoised)


def solution(mesh):
    placed = (
        P("seq", "req", "cfg"),
        P("cfg", "seq", "req", None),
        P("cfg", "seq", "req", None),
        P("cfg", "seq", "req", None),
        P("cfg", "seq", "req", None),
        P("cfg", "seq", "req", None),
        P("cfg", "seq", "req", None),
        P("cfg", "req"),
        P(None, "seq"),
        P("req"),
        P("req"),
        P(("cfg", "seq"), None),
        P("cfg", "req", None),
        P("cfg", "req", None),
        P("cfg", "req", None),
        P(),
        P(),
    )
    return jax.shard_map(
        shards,
        mesh=mesh,
        in_specs=placed,
        out_specs=(P("seq", "req", "cfg"), P("seq", "req", "cfg")),
        check_vma=False,
    )
```
